256 devices in a mesh: ctx: 16 (over y, x), ch: 16 (over z, core).
Axes of the slice: x: 4, y: 4, z: 8, core: 2. Of those that a mesh axis runs over, the one named last changes fastest.
Arguments:
- qkv: bfloat16 [3, 512, 16384], P(None, 'ch', 'ctx'), may hold values from -6 to 6
- short_taps: float32 [3, 512, 7], P(None, 'ch'), may hold values from -2 to 2
- long_filter: float32 [512, 16384], P('ch', 'ctx'), may hold values from -0.046875 to 0.046875
- skip_gain: float32 [512], P('ch'), may hold values from -4 to 4
- out_weight: bfloat16 [8192, 512], P('ch'), may hold values from -0.25 to 0.25
Outputs:
- projected: bfloat16 [8192, 16384], P('ch', 'ctx')
The draws below stay inside these ranges and needn't reach their ends.
All inputs are finite; a program needn't handle non-finite values.
Results may differ from the reference program's by a relative error of at most 0.0049.
Values may be sent and summed in bfloat16 or wider, within the bound.
A program may use at most 64 MiB of HBM per device.

```python
import jax
import jax.numpy as jnp
from jax import lax

DMODEL = 8192
CHANNELS = 512
TAPS = 7
SEQ = 16384


def level_of(stream_key, shape, shards, least, high):
    loudness, own = 1.0, jax.random.fold_in(stream_key, 6)
    for dim, parts in shards:
        steps = jnp.exp(jax.random.uniform(jax.random.fold_in(own, dim), (parts,), jnp.float32, least / len(shards), high / len(shards)))
        loudness = loudness * jnp.repeat(steps, shape[dim] // parts).reshape([-1 if axis == dim else 1 for axis in range(len(shape))])
    return loudness


def gaussian(stream_key, dims, scale, bound, pieces=(), kind=jnp.bfloat16):
    values = jax.random.normal(stream_key, dims, jnp.float32) * scale
    if len(pieces) > 0:
        values = level_of(stream_key, dims, pieces, -0.22, 0.18) * values
    return jnp.clip(values, min=-bound, max=bound).astype(kind)


def setup_inputs(seed: int = 0) -> dict:
    keys = jax.random.split(jax.random.key(seed), 6)
    qkv = gaussian(keys[0], (3, CHANNELS, SEQ), 1.0, 6.0, ((1, 16), (2, 16)))
    short_taps = gaussian(keys[1], (3, CHANNELS, TAPS), TAPS ** -0.5, 2.0, ((1, 16),), jnp.float32)
    long_filter = gaussian(keys[2], (CHANNELS, SEQ), SEQ ** -0.5, 0.046875, ((0, 16), (1, 16)), jnp.float32)
    skip_gain = gaussian(keys[3], (CHANNELS,), 1.0, 4.0, ((0, 16),), jnp.float32)
    out_weight = gaussian(keys[4], (DMODEL, CHANNELS), CHANNELS ** -0.5, 0.25, ((0, 16),))
    return {"qkv": qkv, "short_taps": short_taps, "long_filter": long_filter, "skip_gain": skip_gain, "out_weight": out_weight}


def short_conv(padded, short_taps, length):
    tap_count = short_taps.shape[2]
    result = jnp.zeros(padded.shape[:2] + (length,), jnp.float32)
    for offset in range(tap_count):
        begin_at = tap_count - 1 - offset
        result = result + short_taps[:, :, offset:offset + 1] * padded[:, :, begin_at:begin_at + length]
    return result


def long_conv(signal, kernel):
    length = signal.shape[1]

    def one_group(members):
        sig_rows, ker_rows = members
        spectrum = jnp.fft.rfft(sig_rows, n=2 * length, axis=-1) * jnp.fft.rfft(ker_rows, n=2 * length, axis=-1)
        return jnp.fft.irfft(spectrum, n=2 * length, axis=-1)[:, :length]

    grouped = lax.map(one_group, (signal.reshape(-1, 16, length), kernel.reshape(-1, 16, length)))
    return grouped.reshape(signal.shape)


def reference(qkv, short_taps, long_filter, skip_gain, out_weight):
    tap_count = short_taps.shape[2]
    padded = jnp.pad(qkv.astype(jnp.float32), ((0, 0), (0, 0), (tap_count - 1, 0)))
    featured = short_conv(padded, short_taps, qkv.shape[2])
    product = featured[1] * featured[2]
    mixed = long_conv(product, long_filter) + skip_gain[:, None] * product
    gated = (featured[0] * mixed).astype(jnp.bfloat16)
    return jnp.dot(out_weight, gated, preferred_element_type=jnp.float32).astype(jnp.bfloat16)
```

```python
import functools

import jax
import jax.numpy as jnp
import ml_dtypes
import numpy as np
from jax import lax
from jax.experimental import pallas as pl
from jax.experimental.pallas import tpu as pltpu
from jax.sharding import PartitionSpec as P

MESH = pl.DeviceIdType.MESH
SIDE = 128
TAPS = 7
NODES = 16
ROUND = 8


def split(values):
    high = values.astype(ml_dtypes.bfloat16)
    low = (values - high.astype(np.float64)).astype(ml_dtypes.bfloat16)
    return high, low


def tables():
    k = np.arange(SIDE)[:, None]
    b = np.arange(SIDE)[None, :]
    total = SIDE * SIDE
    first = np.exp(2j * np.pi * (b / (4 * SIDE) - k * b / SIDE))
    twist = np.exp(2j * np.pi * (b / (4 * total) - k * b / total))
    middle = np.exp(-2j * np.pi * k * b / SIDE)
    last = np.conj(first).T / total
    first = np.concatenate([first.real, first.imag], 0)
    first = np.concatenate(split(first), 1)
    forward = np.block([[middle.real, middle.imag], [-middle.imag, middle.real]])
    inverse = np.block([[middle.real, -middle.imag], [middle.imag, middle.real]])
    last = np.concatenate([last.real, -last.imag], 1)
    return (
        first,
        np.stack([twist.real, twist.imag]).astype(np.float32),
        np.stack(split(forward)),
        np.stack(split(inverse)),
        np.stack(split(last)),
    )


def offsets():
    def far(step):
        return min(step, 4 - step)

    steps = [(dy, dx) for dy in range(4) for dx in range(4) if (dy, dx) != (0, 0)]
    return sorted(steps, key=lambda s: -(far(s[0]) + far(s[1])))


def parts(values):
    high = values.astype(jnp.bfloat16)
    return high, (values - high.astype(jnp.float32)).astype(jnp.bfloat16)


def mm(left, right):
    return jnp.dot(left, right, preferred_element_type=jnp.float32)


def kernel(
    qkv_in, taps_in, filt_in, skip_in, first_in, twist_in, fwd_in, inv_in, last_in,
    gath,
    qkv, taps, filt, skip, first, twist, fwd, inv, last,
    wide, send, recv, out_send, out_recv,
    load_sem, tab_sem, a_send, a_recv, q_send, q_recv, b_send, b_recv,
    up_send, up_recv, dn_send, dn_recv, pair_send, pair_recv,
):
    c = lax.axis_index("ctx")
    h = lax.axis_index("ch")
    y, x = c // 4, c % 4
    core = h % 2
    z = h // 2
    partner = h + 1 - 2 * core
    above = ((z + 1) % ROUND) * 2 + core
    below = ((z + ROUND - 1) % ROUND) * 2 + core
    steps = offsets()
    targets = [((y + dy) % 4) * 4 + (x + dx) % 4 for dy, dx in steps]
    sources = [((y + 4 - dy) % 4) * 4 + (x + 4 - dx) % 4 for dy, dx in steps]

    loads = [
        pltpu.make_async_copy(src, dst, load_sem.at[i])
        for i, (src, dst) in enumerate([(qkv_in, qkv), (filt_in, filt)])
    ]
    pairs = [(taps_in, taps), (skip_in, skip), (first_in, first), (twist_in, twist),
             (fwd_in, fwd), (inv_in, inv), (last_in, last)]
    others = [
        pltpu.make_async_copy(src, dst, tab_sem.at[i])
        for i, (src, dst) in enumerate(pairs)
    ]
    for copy in loads:
        copy.start()

    barrier = pltpu.get_barrier_semaphore()
    for target in targets:
        pl.semaphore_signal(barrier, inc=1, device_id={"ctx": target}, device_id_type=MESH)
    for target in (above, below, partner):
        pl.semaphore_signal(barrier, inc=1, device_id={"ch": target}, device_id_type=MESH)
    for copy in others:
        copy.start()
    for copy in loads:
        copy.wait()

    for stream in (1, 2, 3, 0):
        for row in range(8):
            lanes = slice(row * SIDE, (row + 1) * SIDE)
            block = filt[:, lanes] if stream == 3 else qkv[stream, :, lanes]
            wide[pl.ds(row, 32, stride=8), :] = block.astype(jnp.float32)
        send[:, stream] = wide[...].reshape(NODES, 16, SIDE).astype(jnp.bfloat16)

    pl.semaphore_wait(barrier, NODES - 1 + 3)
    a_copies = [
        pltpu.make_async_remote_copy(
            src_ref=send.at[target, 1:4],
            dst_ref=recv.at[c, 1:4],
            send_sem=a_send.at[i],
            recv_sem=a_recv.at[i],
            device_id={"ctx": target},
            device_id_type=MESH,
        )
        for i, target in enumerate(targets)
    ]
    q_copies = [
        pltpu.make_async_remote_copy(
            src_ref=send.at[target, 0:1],
            dst_ref=recv.at[c, 0:1],
            send_sem=q_send.at[i],
            recv_sem=q_recv.at[i],
            device_id={"ctx": target},
            device_id_type=MESH,
        )
        for i, target in enumerate(targets)
    ]
    for copy in a_copies:
        copy.start()
    for copy in q_copies:
        copy.start()
    recv[c] = send[c]
    for copy in others:
        copy.wait()

    lane = lax.broadcasted_iota(jnp.int32, (SIDE, SIDE), 1)
    line = lax.broadcasted_iota(jnp.int32, (SIDE, SIDE), 0)

    def stream_of(stream):
        both = recv[:, stream].astype(jnp.float32).reshape(NODES, 2, 8, SIDE)
        return [both[:, n].reshape(SIDE, SIDE) for n in range(2)]

    def short(values, stream, n):
        before = jnp.where(line == 0, 0.0, pltpu.roll(values, 1, 0))
        tap = taps[stream, pl.ds(2 * c + n, 1), :]
        total = tap[:, 0:1] * values
        for j in range(1, TAPS):
            mixed = jnp.where(lane >= SIDE - j, before, values)
            total = total + tap[:, j : j + 1] * pltpu.roll(mixed, j, 1)
        return total

    twist_re, twist_im = twist[0], twist[1]

    def turned(real, imag):
        return jnp.concatenate(
            [real * twist_re - imag * twist_im, real * twist_im + imag * twist_re], axis=1
        )

    def spectrum(signals):
        data = jnp.concatenate(signals, axis=1)
        head = mm(first[...], jnp.concatenate([data, data], axis=0))
        rows = [
            turned(head[:SIDE, i * SIDE : (i + 1) * SIDE], head[SIDE:, i * SIDE : (i + 1) * SIDE])
            for i in range(len(signals))
        ]
        high, low = parts(jnp.concatenate(rows, axis=0))
        return mm(high, fwd[0]) + mm(low, fwd[0]) + mm(high, fwd[1])

    for copy in a_copies:
        copy.wait_recv()
    filter_rows = recv[:, 3].reshape(NODES, 2, 8, SIDE)
    filters = [filter_rows[:, n].reshape(SIDE, SIDE) for n in range(2)]
    spec_f = spectrum(filters)
    k_rows, v_rows = stream_of(1), stream_of(2)
    product = [short(k_rows[n], 1, n) * short(v_rows[n], 2, n) for n in range(2)]
    spec_p = spectrum([p.astype(jnp.bfloat16) for p in product])
    p_re, p_im = spec_p[:, :SIDE], spec_p[:, SIDE:]
    f_re, f_im = spec_f[:, :SIDE], spec_f[:, SIDE:]
    joined = jnp.concatenate([p_re * f_re - p_im * f_im, p_re * f_im + p_im * f_re], axis=1)
    high, low = parts(joined)
    back = mm(high, inv[0]) + mm(low, inv[0]) + mm(high, inv[1])
    columns = []
    for n in range(2):
        real = back[n * SIDE : (n + 1) * SIDE, :SIDE]
        imag = back[n * SIDE : (n + 1) * SIDE, SIDE:]
        columns.append(
            jnp.concatenate(
                [real * twist_re + imag * twist_im, imag * twist_re - real * twist_im], axis=0
            )
        )
    high, low = parts(jnp.concatenate(columns, axis=1))
    convolved = mm(last[0], high) + mm(last[1], high) + mm(last[0], low)

    for copy in q_copies:
        copy.wait_recv()
    q_rows = stream_of(0)
    gated = []
    for n in range(2):
        query = short(q_rows[n], 0, n)
        mixed = convolved[:, n * SIDE : (n + 1) * SIDE] + skip[2 * c + n] * product[n]
        gated.append((query * mixed).reshape(NODES, 1, 8, SIDE))
    out_send[...] = (
        jnp.concatenate(gated, axis=1).reshape(NODES, 16, SIDE).astype(jnp.bfloat16)
    )

    b_copies = [
        pltpu.make_async_remote_copy(
            src_ref=out_send.at[target],
            dst_ref=out_recv.at[c],
            send_sem=b_send.at[i],
            recv_sem=b_recv.at[i],
            device_id={"ctx": target},
            device_id_type=MESH,
        )
        for i, target in enumerate(targets)
    ]
    for copy in b_copies:
        copy.start()
    out_recv[c] = out_send[c]
    for copy in b_copies:
        copy.wait_recv()

    wide[...] = out_recv[...].astype(jnp.float32).reshape(2 * SIDE, SIDE)
    for row in range(8):
        gath[h, :, row * SIDE : (row + 1) * SIDE] = wide[pl.ds(row, 32, stride=8), :].astype(
            jnp.bfloat16
        )

    def ring(owner, half, send_sem, recv_sem, index, target):
        block = gath.at[owner, pl.ds(half * 16, 16)]
        return pltpu.make_async_remote_copy(
            src_ref=block,
            dst_ref=block,
            send_sem=send_sem.at[index, half],
            recv_sem=recv_sem.at[index, half],
            device_id={"ch": target},
            device_id_type=MESH,
        )

    up_steps, dn_steps = (4, 3), (3, 4)
    started = []
    pair_index = {}

    def to_partner(index, half, owner):
        copy = ring(owner, half, pair_send, pair_recv, index, partner)
        copy.start()
        started.append(copy)

    for half in range(2):
        for copy in (
            ring(h, half, up_send, up_recv, 0, above),
            ring(h, half, dn_send, dn_recv, 0, below),
        ):
            copy.start()
            started.append(copy)
        to_partner(0, half, h)
    for step in range(1, 5):
        for half in range(2):
            for limit, s_sem, r_sem, target, sign in (
                (up_steps[half], up_send, up_recv, above, -1),
                (dn_steps[half], dn_send, dn_recv, below, 1),
            ):
                if step > limit:
                    continue
                owner = ((z + ROUND + sign * step) % ROUND) * 2 + core
                ring(owner, half, s_sem, r_sem, step - 1, target).wait_recv()
                if step < limit:
                    copy = ring(owner, half, s_sem, r_sem, step, target)
                    copy.start()
                    started.append(copy)
                to_partner(step if sign < 0 else 4 + step, half, owner)
    for half in range(2):
        ring(h, half, pair_send, pair_recv, 0, partner).wait_recv()
    for step in range(1, 5):
        for half in range(2):
            for limit, sign in ((up_steps[half], -1), (dn_steps[half], 1)):
                if step > limit:
                    continue
                index = step if sign < 0 else 4 + step
                ring(h, half, pair_send, pair_recv, index, partner).wait_recv()
    for copy in a_copies + q_copies + b_copies + started:
        copy.wait_send()


def solution(mesh):
    consts = tables()
    dma = pltpu.SemaphoreType.DMA
    peers = NODES - 1

    def local(qkv, short_taps, long_filter, skip_gain, out_weight):
        gathered = pl.pallas_call(
            kernel,
            out_shape=jax.ShapeDtypeStruct((NODES, 32, 1024), jnp.bfloat16),
            in_specs=[pl.BlockSpec(memory_space=pl.ANY)] * 9,
            out_specs=pl.BlockSpec(memory_space=pltpu.VMEM),
            scratch_shapes=[
                pltpu.VMEM((3, 32, 1024), jnp.bfloat16),
                pltpu.VMEM((3, 32, TAPS), jnp.float32),
                pltpu.VMEM((32, 1024), jnp.float32),
                pltpu.SMEM((32,), jnp.float32),
                pltpu.VMEM((256, 256), jnp.bfloat16),
                pltpu.VMEM((2, SIDE, SIDE), jnp.float32),
                pltpu.VMEM((2, 256, 256), jnp.bfloat16),
                pltpu.VMEM((2, 256, 256), jnp.bfloat16),
                pltpu.VMEM((2, SIDE, 256), jnp.bfloat16),
                pltpu.VMEM((256, SIDE), jnp.float32),
                pltpu.VMEM((NODES, 4, 16, SIDE), jnp.bfloat16),
                pltpu.VMEM((NODES, 4, 16, SIDE), jnp.bfloat16),
                pltpu.VMEM((NODES, 16, SIDE), jnp.bfloat16),
                pltpu.VMEM((NODES, 16, SIDE), jnp.bfloat16),
                dma((2,)),
                dma((7,)),
                dma((peers,)),
                dma((peers,)),
                dma((peers,)),
                dma((peers,)),
                dma((peers,)),
                dma((peers,)),
                dma((4, 2)),
                dma((4, 2)),
                dma((4, 2)),
                dma((4, 2)),
                dma((9, 2)),
                dma((9, 2)),
            ],
            compiler_params=pltpu.CompilerParams(collective_id=0, has_side_effects=True),
        )(qkv, short_taps, long_filter, skip_gain, *[jnp.asarray(t) for t in consts])
        summed = jnp.dot(
            out_weight,
            gathered.reshape(NODES * 32, 1024),
            preferred_element_type=jnp.float32,
        )
        return summed.astype(jnp.bfloat16)

    placed = (P(None, "ch", "ctx"), P(None, "ch", None), P("ch", "ctx"), P("ch"), P("ch", None))
    return jax.shard_map(
        local, mesh=mesh, in_specs=placed, out_specs=P("ch", "ctx"), check_vma=False
    )
```

```python
import functools

import jax
import jax.numpy as jnp
import ml_dtypes
import numpy as np
from jax import lax
from jax.experimental import pallas as pl
from jax.experimental.pallas import tpu as pltpu
from jax.sharding import PartitionSpec as P

MESH = pl.DeviceIdType.MESH
SIDE = 128
TAPS = 7
NODES = 16
ROUND = 8


def split(values):
    high = values.astype(ml_dtypes.bfloat16)
    low = (values - high.astype(np.float64)).astype(ml_dtypes.bfloat16)
    return high, low


def tables():
    k = np.arange(SIDE)[:, None]
    b = np.arange(SIDE)[None, :]
    total = SIDE * SIDE
    first = np.exp(2j * np.pi * (b / (4 * SIDE) - k * b / SIDE))
    twist = np.exp(2j * np.pi * (b / (4 * total) - k * b / total))
    middle = np.exp(-2j * np.pi * k * b / SIDE)
    last = np.conj(first).T / total
    first = np.concatenate([first.real, first.imag], 0)
    first = np.concatenate(split(first), 1)
    forward = np.block([[middle.real, middle.imag], [-middle.imag, middle.real]])
    inverse = np.block([[middle.real, -middle.imag], [middle.imag, middle.real]])
    last = np.concatenate([last.real, -last.imag], 1)
    return (
        first,
        np.stack([twist.real, twist.imag]).astype(np.float32),
        np.stack(split(forward)),
        np.stack(split(inverse)),
        np.stack(split(last)),
    )


def offsets():
    def far(step):
        return min(step, 4 - step)

    steps = [(dy, dx) for dy in range(4) for dx in range(4) if (dy, dx) != (0, 0)]
    return sorted(steps, key=lambda s: -(far(s[0]) + far(s[1])))


def parts(values):
    high = values.astype(jnp.bfloat16)
    return high, (values - high.astype(jnp.float32)).astype(jnp.bfloat16)


def mm(left, right):
    return jnp.dot(left, right, preferred_element_type=jnp.float32)


def kernel(
    qkv_in, taps_in, filt_in, skip_in, first_in, twist_in, fwd_in, inv_in, last_in,
    gath,
    qkv, taps, filt, skip, first, twist, fwd, inv, last,
    wide, send, recv, out_send, out_recv,
    load_sem, tab_sem, a_send, a_recv, q_send, q_recv, b_send, b_recv,
    z_send, z_recv, pair_send, pair_recv,
):
    c = lax.axis_index("ctx")
    h = lax.axis_index("ch")
    y, x = c // 4, c % 4
    core = h % 2
    z = h // 2
    partner = h + 1 - 2 * core
    def plane(jump):
        return ((z + ROUND + jump) % ROUND) * 2 + core

    steps = offsets()
    targets = [((y + dy) % 4) * 4 + (x + dx) % 4 for dy, dx in steps]
    sources = [((y + 4 - dy) % 4) * 4 + (x + 4 - dx) % 4 for dy, dx in steps]

    sent = []
    loads = [
        pltpu.make_async_copy(src, dst, load_sem.at[i])
        for i, (src, dst) in enumerate([(qkv_in, qkv), (filt_in, filt)])
    ]
    pairs = [(taps_in, taps), (skip_in, skip), (first_in, first), (twist_in, twist),
             (fwd_in, fwd), (inv_in, inv), (last_in, last)]
    others = [
        pltpu.make_async_copy(src, dst, tab_sem.at[i])
        for i, (src, dst) in enumerate(pairs)
    ]
    for copy in loads:
        copy.start()

    barrier = pltpu.get_barrier_semaphore()
    for target in targets:
        pl.semaphore_signal(barrier, inc=1, device_id={"ctx": target}, device_id_type=MESH)
    for jump in (1, -1, 2, -2):
        pl.semaphore_signal(barrier, inc=1, device_id={"ch": plane(jump)}, device_id_type=MESH)
    pl.semaphore_signal(barrier, inc=1, device_id={"ch": partner}, device_id_type=MESH)
    for jump in (2, -2):
        for target in targets:
            pl.semaphore_signal(
                barrier,
                inc=1,
                device_id={"ctx": target, "ch": plane(jump)},
                device_id_type=MESH,
            )
    for copy in others:
        copy.start()
    for copy in loads:
        copy.wait()

    for stream in (1, 2, 3, 0):
        for row in range(8):
            lanes = slice(row * SIDE, (row + 1) * SIDE)
            block = filt[:, lanes] if stream == 3 else qkv[stream, :, lanes]
            wide[pl.ds(row, 32, stride=8), :] = block.astype(jnp.float32)
        send[:, stream] = wide[...].reshape(NODES, 16, SIDE).astype(jnp.bfloat16)

    pl.semaphore_wait(barrier, 3 * (NODES - 1) + 5)
    a_copies = [
        pltpu.make_async_remote_copy(
            src_ref=send.at[target, 1:4],
            dst_ref=recv.at[c, 1:4],
            send_sem=a_send.at[i],
            recv_sem=a_recv.at[i],
            device_id={"ctx": target},
            device_id_type=MESH,
        )
        for i, target in enumerate(targets)
    ]
    q_copies = [
        pltpu.make_async_remote_copy(
            src_ref=send.at[target, 0:1],
            dst_ref=recv.at[c, 0:1],
            send_sem=q_send.at[i],
            recv_sem=q_recv.at[i],
            device_id={"ctx": target},
            device_id_type=MESH,
        )
        for i, target in enumerate(targets)
    ]
    for copy in a_copies:
        copy.start()
    for copy in q_copies:
        copy.start()
    sent += a_copies + q_copies
    recv[c] = send[c]
    for copy in others:
        copy.wait()

    lane = lax.broadcasted_iota(jnp.int32, (SIDE, SIDE), 1)
    spot = lax.broadcasted_iota(jnp.int32, (TAPS, 32), 1)
    line = lax.broadcasted_iota(jnp.int32, (SIDE, SIDE), 0)

    def stream_of(stream):
        both = recv[:, stream].astype(jnp.float32).reshape(NODES, 2, 8, SIDE)
        return [both[:, n].reshape(SIDE, SIDE) for n in range(2)]

    def short(values, stream, n):
        before = jnp.where(line == 0, 0.0, pltpu.roll(values, 1, 0))
        tap = jnp.sum(jnp.where(spot == 2 * c + n, taps[stream], 0.0), axis=1, keepdims=True)
        total = tap[0:1] * values
        for j in range(1, TAPS):
            mixed = jnp.where(lane >= SIDE - j, before, values)
            total = total + tap[j : j + 1] * pltpu.roll(mixed, j, 1)
        return total

    twist_re, twist_im = twist[0], twist[1]

    def turned(real, imag):
        return jnp.concatenate(
            [real * twist_re - imag * twist_im, real * twist_im + imag * twist_re], axis=1
        )

    def spectrum(signals):
        data = jnp.concatenate(signals, axis=1)
        head = mm(first[...], jnp.concatenate([data, data], axis=0))
        rows = [
            turned(head[:SIDE, i * SIDE : (i + 1) * SIDE], head[SIDE:, i * SIDE : (i + 1) * SIDE])
            for i in range(len(signals))
        ]
        high, low = parts(jnp.concatenate(rows, axis=0))
        return mm(high, fwd[0]) + mm(low, fwd[0]) + mm(high, fwd[1])

    for copy in a_copies:
        copy.wait_recv()
    filter_rows = recv[:, 3].reshape(NODES, 2, 8, SIDE)
    filters = [filter_rows[:, n].reshape(SIDE, SIDE) for n in range(2)]
    spec_f = spectrum(filters)
    k_rows, v_rows = stream_of(1), stream_of(2)
    product = [short(k_rows[n], 1, n) * short(v_rows[n], 2, n) for n in range(2)]
    spec_p = spectrum([p.astype(jnp.bfloat16) for p in product])
    p_re, p_im = spec_p[:, :SIDE], spec_p[:, SIDE:]
    f_re, f_im = spec_f[:, :SIDE], spec_f[:, SIDE:]
    joined = jnp.concatenate([p_re * f_re - p_im * f_im, p_re * f_im + p_im * f_re], axis=1)
    high, low = parts(joined)
    back = mm(high, inv[0]) + mm(low, inv[0]) + mm(high, inv[1])
    columns = []
    for n in range(2):
        real = back[n * SIDE : (n + 1) * SIDE, :SIDE]
        imag = back[n * SIDE : (n + 1) * SIDE, SIDE:]
        columns.append(
            jnp.concatenate(
                [real * twist_re + imag * twist_im, imag * twist_re - real * twist_im], axis=0
            )
        )
    high, low = parts(jnp.concatenate(columns, axis=1))
    convolved = mm(last[0], high) + mm(last[1], high) + mm(last[0], low)

    for copy in q_copies:
        copy.wait_recv()
    q_rows = stream_of(0)
    gated = []
    for n in range(2):
        query = short(q_rows[n], 0, n)
        mixed = convolved[:, n * SIDE : (n + 1) * SIDE] + skip[2 * c + n] * product[n]
        gated.append((query * mixed).reshape(NODES, 1, 8, SIDE))
    out_send[...] = (
        jnp.concatenate(gated, axis=1).reshape(NODES, 16, SIDE).astype(jnp.bfloat16)
    )

    jumps = (0, 2, -2)
    b_copies = []
    for group, jump in enumerate(jumps):
        copies = [
            pltpu.make_async_remote_copy(
                src_ref=out_send.at[target],
                dst_ref=out_recv.at[group, c],
                send_sem=b_send.at[group, i],
                recv_sem=b_recv.at[group, i],
                device_id={"ctx": target, "ch": plane(jump)},
                device_id_type=MESH,
            )
            for i, target in enumerate(targets + ([c] if jump else []))
        ]
        b_copies.append(copies)
    for group in (1, 2, 0):
        for copy in b_copies[group]:
            copy.start()
        sent += b_copies[group]
    out_recv[0, c] = out_send[c]

    def hop(owner, part, send_sem, recv_sem, index, target):
        block = gath.at[owner] if part is None else gath.at[owner, pl.ds(part * 16, 16)]
        return pltpu.make_async_remote_copy(
            src_ref=block,
            dst_ref=block,
            send_sem=send_sem.at[index],
            recv_sem=recv_sem.at[index],
            device_id={"ch": target},
            device_id_type=MESH,
        )

    def begin(copy):
        copy.start()
        sent.append(copy)

    def share(index, owner, part=None):
        begin(hop(owner, part, pair_send, pair_recv, index, partner))

    for group, jump in enumerate(jumps):
        for copy in b_copies[group]:
            copy.wait_recv()
        owner = plane(-jump)
        wide[...] = out_recv[group].astype(jnp.float32).reshape(2 * SIDE, SIDE)
        for row in range(8):
            gath[owner, :, row * SIDE : (row + 1) * SIDE] = wide[
                pl.ds(row, 32, stride=8), :
            ].astype(jnp.bfloat16)
        if jump == 0:
            begin(hop(owner, None, z_send, z_recv, 0, plane(1)))
            begin(hop(owner, None, z_send, z_recv, 1, plane(-1)))
        elif jump > 0:
            begin(hop(owner, 0, z_send, z_recv, 4, plane(2)))
            begin(hop(owner, None, z_send, z_recv, 2, plane(1)))
        else:
            begin(hop(owner, 1, z_send, z_recv, 5, plane(-2)))
            begin(hop(owner, None, z_send, z_recv, 3, plane(-1)))
        share(group, owner)
    for index, jump, part in (
        (0, -1, None), (1, 1, None), (2, -3, None), (3, 3, None), (4, 4, 0), (5, 4, 1),
    ):
        owner = plane(jump)
        hop(owner, part, z_send, z_recv, index, plane(1)).wait_recv()
        share(3 + index, owner, part)
    for index, part in enumerate((None,) * 7 + (0, 1)):
        hop(h, part, pair_send, pair_recv, index, partner).wait_recv()
    for copy in sent:
        copy.wait_send()


def project(weight, values, out):
    out[...] = mm(weight[...], values[...]).astype(jnp.bfloat16)


def solution(mesh):
    consts = tables()
    dma = pltpu.SemaphoreType.DMA
    peers = NODES - 1

    def local(qkv, short_taps, long_filter, skip_gain, out_weight):
        gathered = pl.pallas_call(
            kernel,
            out_shape=jax.ShapeDtypeStruct((NODES, 32, 1024), jnp.bfloat16),
            in_specs=[pl.BlockSpec(memory_space=pl.ANY)] * 9,
            out_specs=pl.BlockSpec(memory_space=pltpu.VMEM),
            scratch_shapes=[
                pltpu.VMEM((3, 32, 1024), jnp.bfloat16),
                pltpu.VMEM((3, TAPS, 32), jnp.float32),
                pltpu.VMEM((32, 1024), jnp.float32),
                pltpu.SMEM((32,), jnp.float32),
                pltpu.VMEM((256, 256), jnp.bfloat16),
                pltpu.VMEM((2, SIDE, SIDE), jnp.float32),
                pltpu.VMEM((2, 256, 256), jnp.bfloat16),
                pltpu.VMEM((2, 256, 256), jnp.bfloat16),
                pltpu.VMEM((2, SIDE, 256), jnp.bfloat16),
                pltpu.VMEM((256, SIDE), jnp.float32),
                pltpu.VMEM((NODES, 4, 16, SIDE), jnp.bfloat16),
                pltpu.VMEM((NODES, 4, 16, SIDE), jnp.bfloat16),
                pltpu.VMEM((NODES, 16, SIDE), jnp.bfloat16),
                pltpu.VMEM((3, NODES, 16, SIDE), jnp.bfloat16),
                dma((2,)),
                dma((7,)),
                dma((peers,)),
                dma((peers,)),
                dma((peers,)),
                dma((peers,)),
                dma((3, NODES)),
                dma((3, NODES)),
                dma((6,)),
                dma((6,)),
                dma((9,)),
                dma((9,)),
            ],
            compiler_params=pltpu.CompilerParams(collective_id=0, has_side_effects=True),
        )(qkv, jnp.swapaxes(short_taps, 1, 2), long_filter, skip_gain, *[jnp.asarray(t) for t in consts])
        return pl.pallas_call(
            project,
            grid=(4,),
            out_shape=jax.ShapeDtypeStruct((512, 1024), jnp.bfloat16),
            in_specs=[
                pl.BlockSpec((512, 512), lambda i: (0, 0)),
                pl.BlockSpec((512, 256), lambda i: (0, i)),
            ],
            out_specs=pl.BlockSpec((512, 256), lambda i: (0, i)),
        )(out_weight, gathered.reshape(NODES * 32, 1024))

    placed = (P(None, "ch", "ctx"), P(None, "ch", None), P("ch", "ctx"), P("ch"), P("ch", None))
    return jax.shard_map(
        local, mesh=mesh, in_specs=placed, out_specs=P("ch", "ctx"), check_vma=False
    )
```

```python
import functools

import jax
import jax.numpy as jnp
import ml_dtypes
import numpy as np
from jax import lax
from jax.experimental import pallas as pl
from jax.experimental.pallas import tpu as pltpu
from jax.sharding import PartitionSpec as P

MESH = pl.DeviceIdType.MESH
SIDE = 128
TAPS = 7
NODES = 16
ROUND = 8
GRANT = 16 << 20
CHUNK = 256


def split(values):
    high = values.astype(ml_dtypes.bfloat16)
    low = (values - high.astype(np.float64)).astype(ml_dtypes.bfloat16)
    return high, low


def tables():
    k = np.arange(SIDE)[:, None]
    b = np.arange(SIDE)[None, :]
    total = SIDE * SIDE
    first = np.exp(2j * np.pi * (b / (4 * SIDE) - k * b / SIDE))
    twist = np.exp(2j * np.pi * (b / (4 * total) - k * b / total))
    middle = np.exp(-2j * np.pi * k * b / SIDE)
    last = np.conj(first).T / total
    first = np.concatenate([first.real, first.imag], 0)
    first = np.concatenate(split(first), 1)
    forward = np.block([[middle.real, middle.imag], [-middle.imag, middle.real]])
    inverse = np.block([[middle.real, -middle.imag], [middle.imag, middle.real]])
    last = np.concatenate([last.real, -last.imag], 1)
    return (
        first,
        np.stack([twist.real, twist.imag]).astype(np.float32),
        np.stack(split(forward)),
        np.stack(split(inverse)),
        np.stack(split(last)),
    )


def offsets():
    def far(step):
        return min(step, 4 - step)

    steps = [(dy, dx) for dy in range(4) for dx in range(4) if (dy, dx) != (0, 0)]
    return sorted(steps, key=lambda s: -(far(s[0]) + far(s[1])))


def parts(values):
    high = values.astype(jnp.bfloat16)
    return high, (values - high.astype(jnp.float32)).astype(jnp.bfloat16)


def mm(left, right):
    return jnp.dot(left, right, preferred_element_type=jnp.float32)


def kernel(
    qkv_in, taps_in, filt_in, skip_in, weight_in, first_in, twist_in, fwd_in, inv_in, last_in,
    out,
    qkv, taps, filt, skip, first, twist, fwd, inv, last,
    weight, picked, gath, total, wide, send, recv, out_send, out_recv,
    load_sem, tab_sem, a_send, a_recv, q_send, q_recv, b_send, b_recv,
    z_send, z_recv, pair_send, pair_recv, ready,
):
    c = lax.axis_index("ctx")
    h = lax.axis_index("ch")
    y, x = c // 4, c % 4
    core = h % 2
    z = h // 2
    partner = h + 1 - 2 * core
    def plane(jump):
        return ((z + ROUND + jump) % ROUND) * 2 + core

    steps = offsets()
    targets = [((y + dy) % 4) * 4 + (x + dx) % 4 for dy, dx in steps]
    sources = [((y + 4 - dy) % 4) * 4 + (x + 4 - dx) % 4 for dy, dx in steps]

    sent = []
    loads = [
        pltpu.make_async_copy(src, dst, load_sem.at[i])
        for i, (src, dst) in enumerate([(qkv_in, qkv), (filt_in, filt)])
    ]
    pairs = [(taps_in, taps), (skip_in, skip), (first_in, first), (twist_in, twist),
             (fwd_in, fwd), (inv_in, inv), (last_in, last), (weight_in, weight)]
    others = [
        pltpu.make_async_copy(src, dst, tab_sem.at[i])
        for i, (src, dst) in enumerate(pairs)
    ]
    for copy in loads:
        copy.start()

    barrier = pltpu.get_barrier_semaphore()
    for target in targets:
        pl.semaphore_signal(barrier, inc=1, device_id={"ctx": target}, device_id_type=MESH)
    for jump in (1, -1, 2, -2):
        pl.semaphore_signal(barrier, inc=1, device_id={"ch": plane(jump)}, device_id_type=MESH)
    pl.semaphore_signal(barrier, inc=1, device_id={"ch": partner}, device_id_type=MESH)
    for copy in others:
        copy.start()
    for copy in loads:
        copy.wait()

    for stream in (1, 2, 3, 0):
        for row in range(8):
            lanes = slice(row * SIDE, (row + 1) * SIDE)
            block = filt[:, lanes] if stream == 3 else qkv[stream, :, lanes]
            wide[pl.ds(row, 32, stride=8), :] = block.astype(jnp.float32)
        send[:, stream] = wide[...].reshape(NODES, 16, SIDE).astype(jnp.bfloat16)

    pl.semaphore_wait(barrier, NODES - 1 + 5)
    for jump in (1, -1, 2, -2):
        pl.semaphore_signal(ready, inc=1, device_id={"ch": plane(jump)}, device_id_type=MESH)
    a_copies = [
        pltpu.make_async_remote_copy(
            src_ref=send.at[target, 1:4],
            dst_ref=recv.at[c, 1:4],
            send_sem=a_send.at[i],
            recv_sem=a_recv.at[i],
            device_id={"ctx": target},
            device_id_type=MESH,
        )
        for i, target in enumerate(targets)
    ]
    q_copies = [
        pltpu.make_async_remote_copy(
            src_ref=send.at[target, 0:1],
            dst_ref=recv.at[c, 0:1],
            send_sem=q_send.at[i],
            recv_sem=q_recv.at[i],
            device_id={"ctx": target},
            device_id_type=MESH,
        )
        for i, target in enumerate(targets)
    ]
    for copy in a_copies:
        copy.start()
    for copy in q_copies:
        copy.start()
    sent += a_copies + q_copies
    recv[c] = send[c]
    for copy in others:
        copy.wait()

    wanted = lax.broadcasted_iota(jnp.int32, (512, 512), 1)
    holder = (wanted // 256 + core) % 2
    wanted = (wanted // 32) % ROUND * 64 + holder * 32 + wanted % 32
    given = lax.broadcasted_iota(jnp.int32, (512, 512), 0)
    chosen = jnp.where(given == wanted, 1.0, 0.0).astype(jnp.bfloat16)
    picked[...] = mm(weight[...], chosen).astype(jnp.bfloat16)

    lane = lax.broadcasted_iota(jnp.int32, (SIDE, SIDE), 1)
    spot = lax.broadcasted_iota(jnp.int32, (TAPS, 32), 1)
    line = lax.broadcasted_iota(jnp.int32, (SIDE, SIDE), 0)

    def stream_of(stream):
        both = recv[:, stream].astype(jnp.float32).reshape(NODES, 2, 8, SIDE)
        return [both[:, n].reshape(SIDE, SIDE) for n in range(2)]

    def short(values, stream, n):
        before = jnp.where(line == 0, 0.0, pltpu.roll(values, 1, 0))
        tap = jnp.sum(jnp.where(spot == 2 * c + n, taps[stream], 0.0), axis=1, keepdims=True)
        total = tap[0:1] * values
        for j in range(1, TAPS):
            mixed = jnp.where(lane >= SIDE - j, before, values)
            total = total + tap[j : j + 1] * pltpu.roll(mixed, j, 1)
        return total

    twist_re, twist_im = twist[0], twist[1]

    def turned(real, imag):
        return jnp.concatenate(
            [real * twist_re - imag * twist_im, real * twist_im + imag * twist_re], axis=1
        )

    def spectrum(signals):
        data = jnp.concatenate(signals, axis=1)
        head = mm(first[...], jnp.concatenate([data, data], axis=0))
        rows = [
            turned(head[:SIDE, i * SIDE : (i + 1) * SIDE], head[SIDE:, i * SIDE : (i + 1) * SIDE])
            for i in range(len(signals))
        ]
        high, low = parts(jnp.concatenate(rows, axis=0))
        return mm(high, fwd[0]) + mm(low, fwd[0]) + mm(high, fwd[1])

    for copy in a_copies:
        copy.wait_recv()
    filter_rows = recv[:, 3].reshape(NODES, 2, 8, SIDE)
    filters = [filter_rows[:, n].reshape(SIDE, SIDE) for n in range(2)]
    spec_f = spectrum(filters)
    k_rows, v_rows = stream_of(1), stream_of(2)
    product = [short(k_rows[n], 1, n) * short(v_rows[n], 2, n) for n in range(2)]
    spec_p = spectrum([p.astype(jnp.bfloat16) for p in product])
    p_re, p_im = spec_p[:, :SIDE], spec_p[:, SIDE:]
    f_re, f_im = spec_f[:, :SIDE], spec_f[:, SIDE:]
    joined = jnp.concatenate([p_re * f_re - p_im * f_im, p_re * f_im + p_im * f_re], axis=1)
    high, low = parts(joined)
    back = mm(high, inv[0]) + mm(low, inv[0]) + mm(high, inv[1])
    columns = []
    for n in range(2):
        real = back[n * SIDE : (n + 1) * SIDE, :SIDE]
        imag = back[n * SIDE : (n + 1) * SIDE, SIDE:]
        columns.append(
            jnp.concatenate(
                [real * twist_re + imag * twist_im, imag * twist_re - real * twist_im], axis=0
            )
        )
    high, low = parts(jnp.concatenate(columns, axis=1))
    convolved = mm(last[0], high) + mm(last[1], high) + mm(last[0], low)

    for copy in q_copies:
        copy.wait_recv()
    q_rows = stream_of(0)
    gated = []
    for n in range(2):
        query = short(q_rows[n], 0, n)
        mixed = convolved[:, n * SIDE : (n + 1) * SIDE] + skip[2 * c + n] * product[n]
        gated.append((query * mixed).reshape(NODES, 1, 8, SIDE))
    out_send[...] = (
        jnp.concatenate(gated, axis=1).reshape(NODES, 16, SIDE).astype(jnp.bfloat16)
    )

    jumps = (2, -2, 1, -1, 0)
    pl.semaphore_wait(ready, 4)
    b_copies = []
    for group, jump in enumerate(jumps):
        copies = [
            pltpu.make_async_remote_copy(
                src_ref=out_send.at[target],
                dst_ref=out_recv.at[group, c],
                send_sem=b_send.at[group, i],
                recv_sem=b_recv.at[group, i],
                device_id={"ctx": target, "ch": plane(jump)},
                device_id_type=MESH,
            )
            for i, target in enumerate(targets + ([c] if jump else []))
        ]
        b_copies.append(copies)
    for copies in b_copies:
        for copy in copies:
            copy.start()
        sent += copies
    out_recv[4, c] = out_send[c]

    def hop(height, half, send_sem, recv_sem, index, target, side=0):
        rows = pl.ds(0, 32) if half is None else pl.ds(half * 16, 16)
        return pltpu.make_async_remote_copy(
            src_ref=gath.at[0, height, rows],
            dst_ref=gath.at[side, height, rows],
            send_sem=send_sem.at[index],
            recv_sem=recv_sem.at[index],
            device_id={"ch": target},
            device_id_type=MESH,
        )

    def begin(copy):
        copy.start()
        sent.append(copy)

    def share(index, height, half=None):
        begin(hop(height, half, pair_send, pair_recv, index, partner, 1))

    for group, jump in enumerate(jumps):
        for copy in b_copies[group]:
            copy.wait_recv()
        height = (z + ROUND - jump) % ROUND
        wide[...] = out_recv[group].astype(jnp.float32).reshape(2 * SIDE, SIDE)
        for row in range(8):
            gath[0, height, :, row * SIDE : (row + 1) * SIDE] = wide[
                pl.ds(row, 32, stride=8), :
            ].astype(jnp.bfloat16)
        if jump in (2, -2):
            begin(hop(height, group, z_send, z_recv, 2 + group, plane(jump)))
            begin(hop(height, None, z_send, z_recv, group, plane(jump // 2)))
        share(group, height)
    for index, jump, half in ((0, -3, None), (1, 3, None), (2, 4, 0), (3, 4, 1)):
        height = (z + ROUND + jump) % ROUND
        hop(height, half, z_send, z_recv, index, plane(1)).wait_recv()
        share(5 + index, height, half)
    columns = [slice(i * CHUNK, (i + 1) * CHUNK) for i in range(1024 // CHUNK)]
    for lanes in columns:
        total[:, lanes] = mm(picked[:, :256], gath[0, :, :, lanes].reshape(256, CHUNK))
    for index, half in enumerate((None,) * 7 + (0, 1)):
        hop(z, half, pair_send, pair_recv, index, partner, 1).wait_recv()
    for lanes in columns:
        rest = mm(picked[:, 256:], gath[1, :, :, lanes].reshape(256, CHUNK))
        out[:, lanes] = (total[:, lanes] + rest).astype(jnp.bfloat16)
    for copy in sent:
        copy.wait_send()


def solution(mesh):
    consts = tables()
    dma = pltpu.SemaphoreType.DMA
    peers = NODES - 1

    def local(qkv, short_taps, long_filter, skip_gain, out_weight):
        operands = [qkv, jnp.swapaxes(short_taps, 1, 2), long_filter, skip_gain, out_weight]
        operands += [jnp.asarray(t) for t in consts]
        return pl.pallas_call(
            kernel,
            out_shape=jax.ShapeDtypeStruct((512, 1024), jnp.bfloat16),
            in_specs=[pl.BlockSpec(memory_space=pltpu.HBM)] * 10,
            out_specs=pl.BlockSpec(memory_space=pltpu.VMEM),
            scratch_shapes=[
                pltpu.VMEM((3, 32, 1024), jnp.bfloat16),
                pltpu.VMEM((3, TAPS, 32), jnp.float32),
                pltpu.VMEM((32, 1024), jnp.float32),
                pltpu.SMEM((32,), jnp.float32),
                pltpu.VMEM((256, 256), jnp.bfloat16),
                pltpu.VMEM((2, SIDE, SIDE), jnp.float32),
                pltpu.VMEM((2, 256, 256), jnp.bfloat16),
                pltpu.VMEM((2, 256, 256), jnp.bfloat16),
                pltpu.VMEM((2, SIDE, 256), jnp.bfloat16),
                pltpu.VMEM((512, 512), jnp.bfloat16),
                pltpu.VMEM((512, 512), jnp.bfloat16),
                pltpu.VMEM((2, ROUND, 32, 1024), jnp.bfloat16),
                pltpu.VMEM((512, 1024), jnp.float32),
                pltpu.VMEM((256, SIDE), jnp.float32),
                pltpu.VMEM((NODES, 4, 16, SIDE), jnp.bfloat16),
                pltpu.VMEM((NODES, 4, 16, SIDE), jnp.bfloat16),
                pltpu.VMEM((NODES, 16, SIDE), jnp.bfloat16),
                pltpu.VMEM((5, NODES, 16, SIDE), jnp.bfloat16),
                dma((2,)),
                dma((8,)),
                dma((peers,)),
                dma((peers,)),
                dma((peers,)),
                dma((peers,)),
                dma((5, NODES)),
                dma((5, NODES)),
                dma((4,)),
                dma((4,)),
                dma((9,)),
                dma((9,)),
                pltpu.SemaphoreType.REGULAR,
            ],
            compiler_params=pltpu.CompilerParams(
                collective_id=0, has_side_effects=True, vmem_limit_bytes=GRANT
            ),
        )(*[pltpu.with_memory_space_constraint(v, pltpu.HBM) for v in operands])

    placed = (P(None, "ch", "ctx"), P(None, "ch", None), P("ch", "ctx"), P("ch"), P("ch", None))
    return jax.shard_map(
        local, mesh=mesh, in_specs=placed, out_specs=P("ch", "ctx"), check_vma=False
    )
```

```python
import functools

import jax
import jax.numpy as jnp
import ml_dtypes
import numpy as np
from jax import lax
from jax.experimental import pallas as pl
from jax.experimental.pallas import tpu as pltpu
from jax.sharding import PartitionSpec as P

MESH = pl.DeviceIdType.MESH
SIDE = 128
TAPS = 7
NODES = 16
ROUND = 8
GRANT = 16 << 20
CHUNK = 256


def split(values):
    high = values.astype(ml_dtypes.bfloat16)
    low = (values - high.astype(np.float64)).astype(ml_dtypes.bfloat16)
    return high, low


def tables():
    k = np.arange(SIDE)[:, None]
    b = np.arange(SIDE)[None, :]
    total = SIDE * SIDE
    first = np.exp(2j * np.pi * (b / (4 * SIDE) - k * b / SIDE))
    twist = np.exp(2j * np.pi * (b / (4 * total) - k * b / total))
    middle = np.exp(-2j * np.pi * k * b / SIDE)
    last = np.conj(first).T / total
    first = np.concatenate([first.real, first.imag], 0)
    first = np.concatenate(split(first), 1)
    forward = np.block([[middle.real, middle.imag], [-middle.imag, middle.real]])
    inverse = np.block([[middle.real, -middle.imag], [middle.imag, middle.real]])
    last = np.concatenate([last.real, -last.imag], 1)
    return (
        first,
        np.stack([twist.real, twist.imag]).astype(np.float32),
        np.stack(split(forward)),
        np.stack(split(inverse)),
        np.stack(split(last)),
    )


def offsets():
    def far(step):
        return min(step, 4 - step)

    steps = [(dy, dx) for dy in range(4) for dx in range(4) if (dy, dx) != (0, 0)]
    return sorted(steps, key=lambda s: -(far(s[0]) + far(s[1])))


def parts(values):
    high = values.astype(jnp.bfloat16)
    return high, (values - high.astype(jnp.float32)).astype(jnp.bfloat16)


def mm(left, right):
    return jnp.dot(left, right, preferred_element_type=jnp.float32)


def kernel(
    qkv_in, taps_in, filt_in, skip_in, weight_in, first_in, twist_in, fwd_in, inv_in, last_in,
    out,
    qkv, taps, filt, skip, first, twist, fwd, inv, last,
    weight, picked, gath, total, wide, send, recv, out_send, out_recv,
    load_sem, tab_sem, a_send, a_recv, q_send, q_recv, b_send, b_recv,
    z_send, z_recv, pair_send, pair_recv, ready,
):
    c = lax.axis_index("ctx")
    h = lax.axis_index("ch")
    y, x = c // 4, c % 4
    core = h % 2
    z = h // 2
    partner = h + 1 - 2 * core
    def plane(jump):
        return ((z + ROUND + jump) % ROUND) * 2 + core

    steps = offsets()
    targets = [((y + dy) % 4) * 4 + (x + dx) % 4 for dy, dx in steps]
    sources = [((y + 4 - dy) % 4) * 4 + (x + 4 - dx) % 4 for dy, dx in steps]

    sent = []
    loads = [
        pltpu.make_async_copy(src, dst, load_sem.at[i])
        for i, (src, dst) in enumerate([(qkv_in, qkv), (filt_in, filt)])
    ]
    pairs = [(taps_in, taps), (skip_in, skip), (first_in, first), (twist_in, twist),
             (fwd_in, fwd), (inv_in, inv), (last_in, last), (weight_in, weight)]
    others = [
        pltpu.make_async_copy(src, dst, tab_sem.at[i])
        for i, (src, dst) in enumerate(pairs)
    ]
    for copy in loads:
        copy.start()

    barrier = pltpu.get_barrier_semaphore()
    for target in targets:
        pl.semaphore_signal(barrier, inc=1, device_id={"ctx": target}, device_id_type=MESH)
    for jump in (1, -1, 2, -2):
        for target in (plane(jump), plane(jump) + partner - h):
            pl.semaphore_signal(barrier, inc=1, device_id={"ch": target}, device_id_type=MESH)
    pl.semaphore_signal(barrier, inc=1, device_id={"ch": partner}, device_id_type=MESH)
    for copy in others:
        copy.start()
    for copy in loads:
        copy.wait()

    for stream in (1, 2, 3, 0):
        for row in range(8):
            lanes = slice(row * SIDE, (row + 1) * SIDE)
            block = filt[:, lanes] if stream == 3 else qkv[stream, :, lanes]
            wide[pl.ds(row, 32, stride=8), :] = block.astype(jnp.float32)
        send[:, stream] = wide[...].reshape(NODES, 16, SIDE).astype(jnp.bfloat16)

    pl.semaphore_wait(barrier, NODES - 1 + 9)
    for jump in (1, -1, 2, -2):
        pl.semaphore_signal(ready, inc=1, device_id={"ch": plane(jump)}, device_id_type=MESH)
    a_copies = [
        pltpu.make_async_remote_copy(
            src_ref=send.at[target, 1:4],
            dst_ref=recv.at[c, 1:4],
            send_sem=a_send.at[i],
            recv_sem=a_recv.at[i],
            device_id={"ctx": target},
            device_id_type=MESH,
        )
        for i, target in enumerate(targets)
    ]
    q_copies = [
        pltpu.make_async_remote_copy(
            src_ref=send.at[target, 0:1],
            dst_ref=recv.at[c, 0:1],
            send_sem=q_send.at[i],
            recv_sem=q_recv.at[i],
            device_id={"ctx": target},
            device_id_type=MESH,
        )
        for i, target in enumerate(targets)
    ]
    for copy in a_copies:
        copy.start()
    for copy in q_copies:
        copy.start()
    sent += a_copies + q_copies
    recv[c] = send[c]
    for copy in others:
        copy.wait()

    wanted = lax.broadcasted_iota(jnp.int32, (512, 512), 1)
    holder = (wanted // 256 + core) % 2
    wanted = (wanted // 32) % ROUND * 64 + holder * 32 + wanted % 32
    given = lax.broadcasted_iota(jnp.int32, (512, 512), 0)
    chosen = jnp.where(given == wanted, 1.0, 0.0).astype(jnp.bfloat16)
    picked[...] = mm(weight[...], chosen).astype(jnp.bfloat16)

    lane = lax.broadcasted_iota(jnp.int32, (SIDE, SIDE), 1)
    spot = lax.broadcasted_iota(jnp.int32, (TAPS, 32), 1)
    line = lax.broadcasted_iota(jnp.int32, (SIDE, SIDE), 0)

    def stream_of(stream):
        both = recv[:, stream].astype(jnp.float32).reshape(NODES, 2, 8, SIDE)
        return [both[:, n].reshape(SIDE, SIDE) for n in range(2)]

    def short(values, stream, n):
        before = jnp.where(line == 0, 0.0, pltpu.roll(values, 1, 0))
        tap = jnp.sum(jnp.where(spot == 2 * c + n, taps[stream], 0.0), axis=1, keepdims=True)
        total = tap[0:1] * values
        for j in range(1, TAPS):
            mixed = jnp.where(lane >= SIDE - j, before, values)
            total = total + tap[j : j + 1] * pltpu.roll(mixed, j, 1)
        return total

    twist_re, twist_im = twist[0], twist[1]

    def turned(real, imag):
        return jnp.concatenate(
            [real * twist_re - imag * twist_im, real * twist_im + imag * twist_re], axis=1
        )

    def spectrum(signals):
        data = jnp.concatenate(signals, axis=1)
        head = mm(first[...], jnp.concatenate([data, data], axis=0))
        rows = [
            turned(head[:SIDE, i * SIDE : (i + 1) * SIDE], head[SIDE:, i * SIDE : (i + 1) * SIDE])
            for i in range(len(signals))
        ]
        high, low = parts(jnp.concatenate(rows, axis=0))
        return mm(high, fwd[0]) + mm(low, fwd[0]) + mm(high, fwd[1])

    for copy in a_copies:
        copy.wait_recv()
    filter_rows = recv[:, 3].reshape(NODES, 2, 8, SIDE)
    filters = [filter_rows[:, n].reshape(SIDE, SIDE) for n in range(2)]
    spec_f = spectrum(filters)
    k_rows, v_rows = stream_of(1), stream_of(2)
    product = [short(k_rows[n], 1, n) * short(v_rows[n], 2, n) for n in range(2)]
    spec_p = spectrum([p.astype(jnp.bfloat16) for p in product])
    p_re, p_im = spec_p[:, :SIDE], spec_p[:, SIDE:]
    f_re, f_im = spec_f[:, :SIDE], spec_f[:, SIDE:]
    joined = jnp.concatenate([p_re * f_re - p_im * f_im, p_re * f_im + p_im * f_re], axis=1)
    high, low = parts(joined)
    back = mm(high, inv[0]) + mm(low, inv[0]) + mm(high, inv[1])
    columns = []
    for n in range(2):
        real = back[n * SIDE : (n + 1) * SIDE, :SIDE]
        imag = back[n * SIDE : (n + 1) * SIDE, SIDE:]
        columns.append(
            jnp.concatenate(
                [real * twist_re + imag * twist_im, imag * twist_re - real * twist_im], axis=0
            )
        )
    high, low = parts(jnp.concatenate(columns, axis=1))
    convolved = mm(last[0], high) + mm(last[1], high) + mm(last[0], low)

    for copy in q_copies:
        copy.wait_recv()
    q_rows = stream_of(0)
    gated = []
    for n in range(2):
        query = short(q_rows[n], 0, n)
        mixed = convolved[:, n * SIDE : (n + 1) * SIDE] + skip[2 * c + n] * product[n]
        gated.append((query * mixed).reshape(NODES, 1, 8, SIDE))
    out_send[...] = (
        jnp.concatenate(gated, axis=1).reshape(NODES, 16, SIDE).astype(jnp.bfloat16)
    )

    jumps = (2, -2, 1, -1, 0)
    pl.semaphore_wait(ready, 4)
    b_copies = []
    for group, jump in enumerate(jumps):
        copies = [
            pltpu.make_async_remote_copy(
                src_ref=out_send.at[target],
                dst_ref=out_recv.at[group, c],
                send_sem=b_send.at[group, i],
                recv_sem=b_recv.at[group, c],
                device_id={"ctx": target, "ch": plane(jump)},
                device_id_type=MESH,
            )
            for i, target in enumerate(targets + ([c] if jump else []))
        ]
        b_copies.append(copies)
    for copies in b_copies:
        for copy in copies:
            copy.start()
        sent += copies
    out_recv[4, c] = out_send[c]

    near = y // 2

    def hop(height, half, send_sem, recv_sem, index, target, side=0):
        first = 0 if half is None else pl.multiple_of((near + half) % 2 * 16, 16)
        rows = pl.ds(first, 32 if half is None else 16)
        return pltpu.make_async_remote_copy(
            src_ref=gath.at[0, height, rows],
            dst_ref=gath.at[side, height, rows],
            send_sem=send_sem.at[index],
            recv_sem=recv_sem.at[index],
            device_id={"ch": target},
            device_id_type=MESH,
        )

    def begin(copy):
        copy.start()
        sent.append(copy)

    def share(index, height, half=None):
        begin(hop(height, half, pair_send, pair_recv, index, partner, 1))

    def landed(group, source):
        pltpu.make_async_remote_copy(
            src_ref=out_send.at[0],
            dst_ref=out_recv.at[group, source],
            send_sem=b_send.at[group, 0],
            recv_sem=b_recv.at[group, source],
            device_id={"ctx": targets[0], "ch": h},
            device_id_type=MESH,
        ).wait_recv()

    for half in range(2):
        part = (near + half) % 2
        for group, jump in ((0, 2), (1, -2)):
            for member in range(8):
                landed(group, part * 8 + member)
            height = (z + ROUND - jump) % ROUND
            piece = out_recv[group, pl.ds(part * 8, 8)].astype(jnp.float32)
            rows = wide.at[pl.ds(group * SIDE, SIDE)]
            rows[...] = piece.reshape(SIDE, SIDE)
            first = pl.multiple_of(part * 16, 16)
            for row in range(8):
                gath[0, height, pl.ds(first, 16), row * SIDE : (row + 1) * SIDE] = rows[
                    pl.ds(row, 16, stride=8), :
                ].astype(jnp.bfloat16)
            for side in range(1 + half):
                across = side * (partner - h)
                if half == group:
                    index = 4 + half + 2 * side
                    begin(hop(height, half, z_send, z_recv, index, plane(jump) + across, side))
                index = 2 * half + group if side == 0 else 8 + group
                begin(hop(height, half, z_send, z_recv, index, plane(jump // 2) + across, side))
    for group in (2, 3, 4):
        jump = jumps[group]
        for source in sources if jump == 0 else sources + [c]:
            landed(group, source)
        height = (z + ROUND - jump) % ROUND
        wide[...] = out_recv[group].astype(jnp.float32).reshape(2 * SIDE, SIDE)
        for row in range(8):
            gath[0, height, :, row * SIDE : (row + 1) * SIDE] = wide[
                pl.ds(row, 32, stride=8), :
            ].astype(jnp.bfloat16)
    for group, jump in enumerate(jumps):
        share(group, (z + ROUND - jump) % ROUND)
    arrivals = ((0, -3, 0), (1, 3, 0), (4, 4, 0), (2, -3, 1), (3, 3, 1), (5, 4, 1))
    for order, (index, jump, half) in enumerate(arrivals):
        height = (z + ROUND + jump) % ROUND
        hop(height, half, z_send, z_recv, index, plane(1)).wait_recv()
        if half == 0:
            share(5 + order, height, half)
    columns = [slice(i * CHUNK, (i + 1) * CHUNK) for i in range(1024 // CHUNK)]
    for lanes in columns:
        total[:, lanes] = mm(picked[:, :256], gath[0, :, :, lanes].reshape(256, CHUNK))
    for index in range(8):
        half = None if index < 5 else 0
        hop(z, half, pair_send, pair_recv, index, partner, 1).wait_recv()
    for index in (8, 9, 7):
        hop(z, 1, z_send, z_recv, index, partner, 1).wait_recv()
    for lanes in columns:
        rest = mm(picked[:, 256:], gath[1, :, :, lanes].reshape(256, CHUNK))
        out[:, lanes] = (total[:, lanes] + rest).astype(jnp.bfloat16)
    for copy in sent:
        copy.wait_send()


def solution(mesh):
    consts = tables()
    dma = pltpu.SemaphoreType.DMA
    peers = NODES - 1

    def local(qkv, short_taps, long_filter, skip_gain, out_weight):
        operands = [qkv, jnp.swapaxes(short_taps, 1, 2), long_filter, skip_gain, out_weight]
        operands += [jnp.asarray(t) for t in consts]
        return pl.pallas_call(
            kernel,
            out_shape=jax.ShapeDtypeStruct((512, 1024), jnp.bfloat16),
            in_specs=[pl.BlockSpec(memory_space=pltpu.HBM)] * 10,
            out_specs=pl.BlockSpec(memory_space=pltpu.VMEM),
            scratch_shapes=[
                pltpu.VMEM((3, 32, 1024), jnp.bfloat16),
                pltpu.VMEM((3, TAPS, 32), jnp.float32),
                pltpu.VMEM((32, 1024), jnp.float32),
                pltpu.SMEM((32,), jnp.float32),
                pltpu.VMEM((256, 256), jnp.bfloat16),
                pltpu.VMEM((2, SIDE, SIDE), jnp.float32),
                pltpu.VMEM((2, 256, 256), jnp.bfloat16),
                pltpu.VMEM((2, 256, 256), jnp.bfloat16),
                pltpu.VMEM((2, SIDE, 256), jnp.bfloat16),
                pltpu.VMEM((512, 512), jnp.bfloat16),
                pltpu.VMEM((512, 512), jnp.bfloat16),
                pltpu.VMEM((2, ROUND, 32, 1024), jnp.bfloat16),
                pltpu.VMEM((512, 1024), jnp.float32),
                pltpu.VMEM((256, SIDE), jnp.float32),
                pltpu.VMEM((NODES, 4, 16, SIDE), jnp.bfloat16),
                pltpu.VMEM((NODES, 4, 16, SIDE), jnp.bfloat16),
                pltpu.VMEM((NODES, 16, SIDE), jnp.bfloat16),
                pltpu.VMEM((5, NODES, 16, SIDE), jnp.bfloat16),
                dma((2,)),
                dma((8,)),
                dma((peers,)),
                dma((peers,)),
                dma((peers,)),
                dma((peers,)),
                dma((5, NODES)),
                dma((5, NODES)),
                dma((10,)),
                dma((10,)),
                dma((8,)),
                dma((8,)),
                pltpu.SemaphoreType.REGULAR,
            ],
            compiler_params=pltpu.CompilerParams(
                collective_id=0, has_side_effects=True, vmem_limit_bytes=GRANT
            ),
        )(*[pltpu.with_memory_space_constraint(v, pltpu.HBM) for v in operands])

    placed = (P(None, "ch", "ctx"), P(None, "ch", None), P("ch", "ctx"), P("ch"), P("ch", None))
    return jax.shard_map(
        local, mesh=mesh, in_specs=placed, out_specs=P("ch", "ctx"), check_vma=False
    )
```

```python
import functools

import jax
import jax.numpy as jnp
import ml_dtypes
import numpy as np
from jax import lax
from jax.experimental import pallas as pl
from jax.experimental.pallas import tpu as pltpu
from jax.sharding import PartitionSpec as P

MESH = pl.DeviceIdType.MESH
SIDE = 128
TAPS = 7
NODES = 16
ROUND = 8
GRANT = 16 << 20
CHUNK = 256


def split(values):
    high = values.astype(ml_dtypes.bfloat16)
    low = (values - high.astype(np.float64)).astype(ml_dtypes.bfloat16)
    return high, low


def tables():
    k = np.arange(SIDE)[:, None]
    b = np.arange(SIDE)[None, :]
    total = SIDE * SIDE
    first = np.exp(2j * np.pi * (b / (4 * SIDE) - k * b / SIDE))
    twist = np.exp(2j * np.pi * (b / (4 * total) - k * b / total))
    middle = np.exp(-2j * np.pi * k * b / SIDE)
    last = np.conj(first).T / total
    first = np.concatenate([first.real, first.imag], 0)
    first = np.concatenate(split(first), 1)
    forward = np.block([[middle.real, middle.imag], [-middle.imag, middle.real]])
    inverse = np.block([[middle.real, -middle.imag], [middle.imag, middle.real]])
    last = np.concatenate([last.real, -last.imag], 1)
    return (
        first,
        np.stack([twist.real, twist.imag]).astype(np.float32),
        np.stack(split(forward)),
        np.stack(split(inverse)),
        np.stack(split(last)),
    )


def offsets():
    def far(step):
        return min(step, 4 - step)

    steps = [(dy, dx) for dy in range(4) for dx in range(4) if (dy, dx) != (0, 0)]
    return sorted(steps, key=lambda s: -(far(s[0]) + far(s[1])))


def parts(values):
    high = values.astype(jnp.bfloat16)
    return high, (values - high.astype(jnp.float32)).astype(jnp.bfloat16)


def mm(left, right):
    return jnp.dot(left, right, preferred_element_type=jnp.float32)


def kernel(
    qkv_in, taps_in, filt_in, skip_in, weight_in, first_in, twist_in, fwd_in, inv_in, last_in,
    total, picked_rest, rest,
    qkv, taps, filt, skip, first, twist, fwd, inv, last,
    weight, picked, gath, wide, send, recv, out_send, out_recv,
    load_sem, tab_sem, a_send, a_recv, q_send, q_recv, b_send, b_recv,
    z_send, z_recv, pair_send, pair_recv, ready,
):
    c = lax.axis_index("ctx")
    h = lax.axis_index("ch")
    y, x = c // 4, c % 4
    core = h % 2
    z = h // 2
    partner = h + 1 - 2 * core
    def plane(jump):
        return ((z + ROUND + jump) % ROUND) * 2 + core

    steps = offsets()
    targets = [((y + dy) % 4) * 4 + (x + dx) % 4 for dy, dx in steps]
    sources = [((y + 4 - dy) % 4) * 4 + (x + 4 - dx) % 4 for dy, dx in steps]

    sent = []
    loads = [
        pltpu.make_async_copy(src, dst, load_sem.at[i])
        for i, (src, dst) in enumerate([(qkv_in, qkv), (filt_in, filt)])
    ]
    pairs = [(taps_in, taps), (skip_in, skip), (first_in, first), (twist_in, twist),
             (fwd_in, fwd), (inv_in, inv), (last_in, last), (weight_in, weight)]
    others = [
        pltpu.make_async_copy(src, dst, tab_sem.at[i])
        for i, (src, dst) in enumerate(pairs)
    ]
    for copy in loads:
        copy.start()

    barrier = pltpu.get_barrier_semaphore()
    for target in targets:
        pl.semaphore_signal(barrier, inc=1, device_id={"ctx": target}, device_id_type=MESH)
    for jump in (1, -1, 2, -2):
        for target in (plane(jump), plane(jump) + partner - h):
            pl.semaphore_signal(barrier, inc=1, device_id={"ch": target}, device_id_type=MESH)
    pl.semaphore_signal(barrier, inc=1, device_id={"ch": partner}, device_id_type=MESH)
    for copy in others:
        copy.start()
    for copy in loads:
        copy.wait()

    for stream in (1, 2, 3, 0):
        for row in range(8):
            lanes = slice(row * SIDE, (row + 1) * SIDE)
            block = filt[:, lanes] if stream == 3 else qkv[stream, :, lanes]
            wide[pl.ds(row, 32, stride=8), :] = block.astype(jnp.float32)
        send[:, stream] = wide[...].reshape(NODES, 16, SIDE).astype(jnp.bfloat16)

    pl.semaphore_wait(barrier, NODES - 1 + 9)
    for jump in (1, -1, 2, -2):
        pl.semaphore_signal(ready, inc=1, device_id={"ch": plane(jump)}, device_id_type=MESH)
    a_copies = [
        pltpu.make_async_remote_copy(
            src_ref=send.at[target, 1:4],
            dst_ref=recv.at[c, 1:4],
            send_sem=a_send.at[i],
            recv_sem=a_recv.at[i],
            device_id={"ctx": target},
            device_id_type=MESH,
        )
        for i, target in enumerate(targets)
    ]
    q_copies = [
        pltpu.make_async_remote_copy(
            src_ref=send.at[target, 0:1],
            dst_ref=recv.at[c, 0:1],
            send_sem=q_send.at[i],
            recv_sem=q_recv.at[i],
            device_id={"ctx": target},
            device_id_type=MESH,
        )
        for i, target in enumerate(targets)
    ]
    for copy in a_copies:
        copy.start()
    for copy in q_copies:
        copy.start()
    sent += a_copies + q_copies
    recv[c] = send[c]
    for copy in others:
        copy.wait()

    wanted = lax.broadcasted_iota(jnp.int32, (512, 512), 1)
    holder = (wanted // 256 + core) % 2
    wanted = (wanted // 32) % ROUND * 64 + holder * 32 + wanted % 32
    given = lax.broadcasted_iota(jnp.int32, (512, 512), 0)
    chosen = jnp.where(given == wanted, 1.0, 0.0).astype(jnp.bfloat16)
    ordered = mm(weight[...], chosen).astype(jnp.bfloat16)
    picked[...] = ordered[:, :256]
    picked_rest[...] = ordered[:, 256:]

    lane = lax.broadcasted_iota(jnp.int32, (SIDE, SIDE), 1)
    spot = lax.broadcasted_iota(jnp.int32, (TAPS, 32), 1)
    line = lax.broadcasted_iota(jnp.int32, (SIDE, SIDE), 0)

    def stream_of(stream):
        both = recv[:, stream].astype(jnp.float32).reshape(NODES, 2, 8, SIDE)
        return [both[:, n].reshape(SIDE, SIDE) for n in range(2)]

    def short(values, stream, n):
        before = jnp.where(line == 0, 0.0, pltpu.roll(values, 1, 0))
        tap = jnp.sum(jnp.where(spot == 2 * c + n, taps[stream], 0.0), axis=1, keepdims=True)
        total = tap[0:1] * values
        for j in range(1, TAPS):
            mixed = jnp.where(lane >= SIDE - j, before, values)
            total = total + tap[j : j + 1] * pltpu.roll(mixed, j, 1)
        return total

    twist_re, twist_im = twist[0], twist[1]

    def turned(real, imag):
        return jnp.concatenate(
            [real * twist_re - imag * twist_im, real * twist_im + imag * twist_re], axis=1
        )

    def spectrum(signals):
        data = jnp.concatenate(signals, axis=1)
        head = mm(first[...], jnp.concatenate([data, data], axis=0))
        rows = [
            turned(head[:SIDE, i * SIDE : (i + 1) * SIDE], head[SIDE:, i * SIDE : (i + 1) * SIDE])
            for i in range(len(signals))
        ]
        high, low = parts(jnp.concatenate(rows, axis=0))
        return mm(high, fwd[0]) + mm(low, fwd[0]) + mm(high, fwd[1])

    for copy in a_copies:
        copy.wait_recv()
    filter_rows = recv[:, 3].reshape(NODES, 2, 8, SIDE)
    filters = [filter_rows[:, n].reshape(SIDE, SIDE) for n in range(2)]
    spec_f = spectrum(filters)
    k_rows, v_rows = stream_of(1), stream_of(2)
    product = [short(k_rows[n], 1, n) * short(v_rows[n], 2, n) for n in range(2)]
    spec_p = spectrum([p.astype(jnp.bfloat16) for p in product])
    p_re, p_im = spec_p[:, :SIDE], spec_p[:, SIDE:]
    f_re, f_im = spec_f[:, :SIDE], spec_f[:, SIDE:]
    joined = jnp.concatenate([p_re * f_re - p_im * f_im, p_re * f_im + p_im * f_re], axis=1)
    high, low = parts(joined)
    back = mm(high, inv[0]) + mm(low, inv[0]) + mm(high, inv[1])
    columns = []
    for n in range(2):
        real = back[n * SIDE : (n + 1) * SIDE, :SIDE]
        imag = back[n * SIDE : (n + 1) * SIDE, SIDE:]
        columns.append(
            jnp.concatenate(
                [real * twist_re + imag * twist_im, imag * twist_re - real * twist_im], axis=0
            )
        )
    high, low = parts(jnp.concatenate(columns, axis=1))
    convolved = mm(last[0], high) + mm(last[1], high) + mm(last[0], low)

    for copy in q_copies:
        copy.wait_recv()
    q_rows = stream_of(0)
    gated = []
    for n in range(2):
        query = short(q_rows[n], 0, n)
        mixed = convolved[:, n * SIDE : (n + 1) * SIDE] + skip[2 * c + n] * product[n]
        gated.append((query * mixed).reshape(NODES, 1, 8, SIDE))
    out_send[...] = (
        jnp.concatenate(gated, axis=1).reshape(NODES, 16, SIDE).astype(jnp.bfloat16)
    )

    jumps = (2, -2, 1, -1, 0)
    pl.semaphore_wait(ready, 4)
    b_copies = []
    for group, jump in enumerate(jumps):
        copies = [
            pltpu.make_async_remote_copy(
                src_ref=out_send.at[target],
                dst_ref=out_recv.at[group, c],
                send_sem=b_send.at[group, i],
                recv_sem=b_recv.at[group, c],
                device_id={"ctx": target, "ch": plane(jump)},
                device_id_type=MESH,
            )
            for i, target in enumerate(targets + ([c] if jump else []))
        ]
        b_copies.append(copies)
    for copies in b_copies:
        for copy in copies:
            copy.start()
        sent += copies
    out_recv[4, c] = out_send[c]

    near = y // 2

    def hop(height, half, send_sem, recv_sem, index, target, side=0):
        first = 0 if half is None else pl.multiple_of((near + half) % 2 * 16, 16)
        rows = pl.ds(first, 32 if half is None else 16)
        return pltpu.make_async_remote_copy(
            src_ref=gath.at[height, rows],
            dst_ref=(gath, rest)[side].at[height, rows],
            send_sem=send_sem.at[index],
            recv_sem=recv_sem.at[index],
            device_id={"ch": target},
            device_id_type=MESH,
        )

    def begin(copy):
        copy.start()
        sent.append(copy)

    def share(index, height, half=None):
        begin(hop(height, half, pair_send, pair_recv, index, partner, 1))

    def landed(group, source):
        pltpu.make_async_remote_copy(
            src_ref=out_send.at[0],
            dst_ref=out_recv.at[group, source],
            send_sem=b_send.at[group, 0],
            recv_sem=b_recv.at[group, source],
            device_id={"ctx": targets[0], "ch": h},
            device_id_type=MESH,
        ).wait_recv()

    for half in range(2):
        part = (near + half) % 2
        for group, jump in ((0, 2), (1, -2)):
            for member in range(8):
                landed(group, part * 8 + member)
            height = (z + ROUND - jump) % ROUND
            piece = out_recv[group, pl.ds(part * 8, 8)].astype(jnp.float32)
            rows = wide.at[pl.ds(group * SIDE, SIDE)]
            rows[...] = piece.reshape(SIDE, SIDE)
            first = pl.multiple_of(part * 16, 16)
            for row in range(8):
                gath[height, pl.ds(first, 16), row * SIDE : (row + 1) * SIDE] = rows[
                    pl.ds(row, 16, stride=8), :
                ].astype(jnp.bfloat16)
            for side in range(1 + half):
                across = side * (partner - h)
                if half == group:
                    index = 4 + half + 2 * side
                    begin(hop(height, half, z_send, z_recv, index, plane(jump) + across, side))
                index = 2 * half + group if side == 0 else 8 + group
                begin(hop(height, half, z_send, z_recv, index, plane(jump // 2) + across, side))
    for group in (2, 3, 4):
        jump = jumps[group]
        for source in sources if jump == 0 else sources + [c]:
            landed(group, source)
        height = (z + ROUND - jump) % ROUND
        wide[...] = out_recv[group].astype(jnp.float32).reshape(2 * SIDE, SIDE)
        for row in range(8):
            gath[height, :, row * SIDE : (row + 1) * SIDE] = wide[
                pl.ds(row, 32, stride=8), :
            ].astype(jnp.bfloat16)
    for group, jump in enumerate(jumps):
        share(group, (z + ROUND - jump) % ROUND)
    arrivals = ((0, -3, 0), (1, 3, 0), (4, 4, 0), (2, -3, 1), (3, 3, 1), (5, 4, 1))
    for order, (index, jump, half) in enumerate(arrivals):
        height = (z + ROUND + jump) % ROUND
        hop(height, half, z_send, z_recv, index, plane(1)).wait_recv()
        if half == 0:
            share(5 + order, height, half)
    columns = [slice(i * CHUNK, (i + 1) * CHUNK) for i in range(1024 // CHUNK)]
    for lanes in columns:
        total[:, lanes] = mm(picked[...], gath[:, :, lanes].reshape(256, CHUNK))
    for index in range(8):
        half = None if index < 5 else 0
        hop(z, half, pair_send, pair_recv, index, partner, 1).wait_recv()
    for index in (8, 9, 7):
        hop(z, 1, z_send, z_recv, index, partner, 1).wait_recv()
    for copy in sent:
        copy.wait_send()


def finish(total, picked, values, out, stage, sem):
    copies = []
    for i in range(1024 // CHUNK):
        rows = pl.ds(i * (512 * CHUNK // 1024), 512 * CHUNK // 1024)
        late = mm(picked[rows, :], values[...])
        stage[rows, :] = (total[rows, :] + late).astype(jnp.bfloat16)
        copy = pltpu.make_async_copy(stage.at[rows], out.at[rows], sem.at[i])
        copy.start()
        copies.append(copy)
    for copy in copies:
        copy.wait()


def solution(mesh):
    consts = tables()
    dma = pltpu.SemaphoreType.DMA
    peers = NODES - 1

    def local(qkv, short_taps, long_filter, skip_gain, out_weight):
        operands = [qkv, jnp.swapaxes(short_taps, 1, 2), long_filter, skip_gain, out_weight]
        operands += [jnp.asarray(t) for t in consts]
        total, picked, rest = pl.pallas_call(
            kernel,
            out_shape=(
                jax.ShapeDtypeStruct((512, 1024), jnp.float32),
                jax.ShapeDtypeStruct((512, 256), jnp.bfloat16),
                jax.ShapeDtypeStruct((ROUND, 32, 1024), jnp.bfloat16),
            ),
            in_specs=[pl.BlockSpec(memory_space=pltpu.HBM)] * 10,
            out_specs=[pl.BlockSpec(memory_space=pltpu.VMEM)] * 3,
            scratch_shapes=[
                pltpu.VMEM((3, 32, 1024), jnp.bfloat16),
                pltpu.VMEM((3, TAPS, 32), jnp.float32),
                pltpu.VMEM((32, 1024), jnp.float32),
                pltpu.SMEM((32,), jnp.float32),
                pltpu.VMEM((256, 256), jnp.bfloat16),
                pltpu.VMEM((2, SIDE, SIDE), jnp.float32),
                pltpu.VMEM((2, 256, 256), jnp.bfloat16),
                pltpu.VMEM((2, 256, 256), jnp.bfloat16),
                pltpu.VMEM((2, SIDE, 256), jnp.bfloat16),
                pltpu.VMEM((512, 512), jnp.bfloat16),
                pltpu.VMEM((512, 256), jnp.bfloat16),
                pltpu.VMEM((ROUND, 32, 1024), jnp.bfloat16),
                pltpu.VMEM((256, SIDE), jnp.float32),
                pltpu.VMEM((NODES, 4, 16, SIDE), jnp.bfloat16),
                pltpu.VMEM((NODES, 4, 16, SIDE), jnp.bfloat16),
                pltpu.VMEM((NODES, 16, SIDE), jnp.bfloat16),
                pltpu.VMEM((5, NODES, 16, SIDE), jnp.bfloat16),
                dma((2,)),
                dma((8,)),
                dma((peers,)),
                dma((peers,)),
                dma((peers,)),
                dma((peers,)),
                dma((5, NODES)),
                dma((5, NODES)),
                dma((10,)),
                dma((10,)),
                dma((8,)),
                dma((8,)),
                pltpu.SemaphoreType.REGULAR,
            ],
            compiler_params=pltpu.CompilerParams(
                collective_id=0, has_side_effects=True, vmem_limit_bytes=GRANT
            ),
        )(*[pltpu.with_memory_space_constraint(v, pltpu.HBM) for v in operands])
        return pl.pallas_call(
            finish,
            out_shape=jax.ShapeDtypeStruct((512, 1024), jnp.bfloat16),
            in_specs=[pl.BlockSpec(memory_space=pltpu.VMEM)] * 3,
            out_specs=pl.BlockSpec(memory_space=pl.ANY),
            scratch_shapes=[pltpu.VMEM((512, 1024), jnp.bfloat16), dma((1024 // CHUNK,))],
            compiler_params=pltpu.CompilerParams(vmem_limit_bytes=GRANT),
        )(total, picked, rest.reshape(256, 1024))

    placed = (P(None, "ch", "ctx"), P(None, "ch", None), P("ch", "ctx"), P("ch"), P("ch", None))
    return jax.shard_map(
        local, mesh=mesh, in_specs=placed, out_specs=P("ch", "ctx"), check_vma=False
    )
```

```python
import functools

import jax
import jax.numpy as jnp
import ml_dtypes
import numpy as np
from jax import lax
from jax.experimental import pallas as pl
from jax.experimental.pallas import tpu as pltpu
from jax.sharding import PartitionSpec as P

MESH = pl.DeviceIdType.MESH
SIDE = 128
TAPS = 7
NODES = 16
ROUND = 8
GRANT = 16 << 20
CHUNK = 256


def split(values):
    high = values.astype(ml_dtypes.bfloat16)
    low = (values - high.astype(np.float64)).astype(ml_dtypes.bfloat16)
    return high, low


def tables():
    k = np.arange(SIDE)[:, None]
    b = np.arange(SIDE)[None, :]
    total = SIDE * SIDE
    first = np.exp(2j * np.pi * (b / (4 * SIDE) - k * b / SIDE))
    twist = np.exp(2j * np.pi * (b / (4 * total) - k * b / total))
    middle = np.exp(-2j * np.pi * k * b / SIDE)
    last = np.conj(first).T / total
    first = np.concatenate([first.real, first.imag], 0)
    first = np.concatenate(split(first), 1)
    forward = np.block([[middle.real, middle.imag], [-middle.imag, middle.real]])
    inverse = np.block([[middle.real, -middle.imag], [middle.imag, middle.real]])
    last = np.concatenate([last.real, -last.imag], 1)
    return (
        first,
        np.stack([twist.real, twist.imag]).astype(np.float32),
        np.stack(split(forward)),
        np.stack(split(inverse)),
        np.stack(split(last)),
    )


def offsets():
    def far(step):
        return min(step, 4 - step)

    steps = [(dy, dx) for dy in range(4) for dx in range(4) if (dy, dx) != (0, 0)]
    return sorted(steps, key=lambda s: -(far(s[0]) + far(s[1])))


def parts(values):
    high = values.astype(jnp.bfloat16)
    return high, (values - high.astype(jnp.float32)).astype(jnp.bfloat16)


def mm(left, right):
    return jnp.dot(left, right, preferred_element_type=jnp.float32)


def kernel(
    qkv_in, taps_in, filt_in, skip_in, weight_in, first_in, twist_in, fwd_in, inv_in, last_in,
    out,
    qkv, taps, filt, skip, first, twist, fwd, inv, last,
    weight, picked, gath, total, wide, send, recv, out_send, out_recv,
    load_sem, tab_sem, a_send, a_recv, q_send, q_recv, b_send, b_recv,
    z_send, z_recv, pair_send, pair_recv, ready,
):
    c = lax.axis_index("ctx")
    h = lax.axis_index("ch")
    y, x = c // 4, c % 4
    core = h % 2
    z = h // 2
    partner = h + 1 - 2 * core
    def plane(jump):
        return ((z + ROUND + jump) % ROUND) * 2 + core

    steps = offsets()
    targets = [((y + dy) % 4) * 4 + (x + dx) % 4 for dy, dx in steps]
    sources = [((y + 4 - dy) % 4) * 4 + (x + 4 - dx) % 4 for dy, dx in steps]

    sent = []
    loads = [
        pltpu.make_async_copy(src, dst, load_sem.at[i])
        for i, (src, dst) in enumerate([(qkv_in, qkv), (filt_in, filt)])
    ]
    pairs = [(taps_in, taps), (skip_in, skip), (first_in, first), (twist_in, twist),
             (fwd_in, fwd), (inv_in, inv), (last_in, last), (weight_in, weight)]
    others = [
        pltpu.make_async_copy(src, dst, tab_sem.at[i])
        for i, (src, dst) in enumerate(pairs)
    ]
    for copy in loads:
        copy.start()

    barrier = pltpu.get_barrier_semaphore()
    for target in targets:
        pl.semaphore_signal(barrier, inc=1, device_id={"ctx": target}, device_id_type=MESH)
    for jump in (1, -1, 2, -2):
        for target in (plane(jump), plane(jump) + partner - h):
            pl.semaphore_signal(barrier, inc=1, device_id={"ch": target}, device_id_type=MESH)
    pl.semaphore_signal(barrier, inc=1, device_id={"ch": partner}, device_id_type=MESH)
    for copy in others:
        copy.start()
    for copy in loads:
        copy.wait()

    for stream in (1, 2, 3, 0):
        for row in range(8):
            lanes = slice(row * SIDE, (row + 1) * SIDE)
            block = filt[:, lanes] if stream == 3 else qkv[stream, :, lanes]
            wide[pl.ds(row, 32, stride=8), :] = block.astype(jnp.float32)
        send[:, stream] = wide[...].reshape(NODES, 16, SIDE).astype(jnp.bfloat16)

    pl.semaphore_wait(barrier, NODES - 1 + 9)
    for jump in (1, -1, 2, -2):
        pl.semaphore_signal(ready, inc=1, device_id={"ch": plane(jump)}, device_id_type=MESH)
    a_copies = [
        pltpu.make_async_remote_copy(
            src_ref=send.at[target, 1:4],
            dst_ref=recv.at[c, 1:4],
            send_sem=a_send.at[i],
            recv_sem=a_recv.at[i],
            device_id={"ctx": target},
            device_id_type=MESH,
        )
        for i, target in enumerate(targets)
    ]
    q_copies = [
        pltpu.make_async_remote_copy(
            src_ref=send.at[target, 0:1],
            dst_ref=recv.at[c, 0:1],
            send_sem=q_send.at[i],
            recv_sem=q_recv.at[i],
            device_id={"ctx": target},
            device_id_type=MESH,
        )
        for i, target in enumerate(targets)
    ]
    for copy in a_copies:
        copy.start()
    for copy in q_copies:
        copy.start()
    sent += a_copies + q_copies
    recv[c] = send[c]
    for copy in others:
        copy.wait()

    wanted = lax.broadcasted_iota(jnp.int32, (512, 512), 1)
    holder = (wanted // 256 + core) % 2
    wanted = (wanted // 32) % ROUND * 64 + holder * 32 + wanted % 32
    given = lax.broadcasted_iota(jnp.int32, (512, 512), 0)
    chosen = jnp.where(given == wanted, 1.0, 0.0).astype(jnp.bfloat16)
    picked[...] = mm(weight[...], chosen).astype(jnp.bfloat16)

    lane = lax.broadcasted_iota(jnp.int32, (SIDE, SIDE), 1)
    spot = lax.broadcasted_iota(jnp.int32, (TAPS, 32), 1)
    line = lax.broadcasted_iota(jnp.int32, (SIDE, SIDE), 0)

    def stream_of(stream):
        both = recv[:, stream].astype(jnp.float32).reshape(NODES, 2, 8, SIDE)
        return [both[:, n].reshape(SIDE, SIDE) for n in range(2)]

    def short(values, stream, n):
        before = jnp.where(line == 0, 0.0, pltpu.roll(values, 1, 0))
        tap = jnp.sum(jnp.where(spot == 2 * c + n, taps[stream], 0.0), axis=1, keepdims=True)
        total = tap[0:1] * values
        for j in range(1, TAPS):
            mixed = jnp.where(lane >= SIDE - j, before, values)
            total = total + tap[j : j + 1] * pltpu.roll(mixed, j, 1)
        return total

    twist_re, twist_im = twist[0], twist[1]

    def turned(real, imag):
        return jnp.concatenate(
            [real * twist_re - imag * twist_im, real * twist_im + imag * twist_re], axis=1
        )

    def spectrum(signals):
        data = jnp.concatenate(signals, axis=1)
        head = mm(first[...], jnp.concatenate([data, data], axis=0))
        rows = [
            turned(head[:SIDE, i * SIDE : (i + 1) * SIDE], head[SIDE:, i * SIDE : (i + 1) * SIDE])
            for i in range(len(signals))
        ]
        high, low = parts(jnp.concatenate(rows, axis=0))
        return mm(high, fwd[0]) + mm(low, fwd[0]) + mm(high, fwd[1])

    for copy in a_copies:
        copy.wait_recv()
    filter_rows = recv[:, 3].reshape(NODES, 2, 8, SIDE)
    filters = [filter_rows[:, n].reshape(SIDE, SIDE) for n in range(2)]
    spec_f = spectrum(filters)
    k_rows, v_rows = stream_of(1), stream_of(2)
    product = [short(k_rows[n], 1, n) * short(v_rows[n], 2, n) for n in range(2)]
    spec_p = spectrum([p.astype(jnp.bfloat16) for p in product])
    for copy in q_copies:
        copy.wait_recv()
    q_rows = stream_of(0)
    queries = [short(q_rows[n], 0, n) for n in range(2)]
    p_re, p_im = spec_p[:, :SIDE], spec_p[:, SIDE:]
    f_re, f_im = spec_f[:, :SIDE], spec_f[:, SIDE:]
    joined = jnp.concatenate([p_re * f_re - p_im * f_im, p_re * f_im + p_im * f_re], axis=1)
    high, low = parts(joined)
    back = mm(high, inv[0]) + mm(low, inv[0]) + mm(high, inv[1])
    columns = []
    for n in range(2):
        real = back[n * SIDE : (n + 1) * SIDE, :SIDE]
        imag = back[n * SIDE : (n + 1) * SIDE, SIDE:]
        columns.append(
            jnp.concatenate(
                [real * twist_re + imag * twist_im, imag * twist_re - real * twist_im], axis=0
            )
        )
    high, low = parts(jnp.concatenate(columns, axis=1))
    convolved = mm(last[0], high) + mm(last[1], high) + mm(last[0], low)

    gated = []
    for n in range(2):
        mixed = convolved[:, n * SIDE : (n + 1) * SIDE] + skip[2 * c + n] * product[n]
        gated.append((queries[n] * mixed).reshape(NODES, 1, 8, SIDE))
    out_send[...] = (
        jnp.concatenate(gated, axis=1).reshape(NODES, 16, SIDE).astype(jnp.bfloat16)
    )

    jumps = (2, -2, 1, -1, 0)
    pl.semaphore_wait(ready, 4)
    b_copies = []
    for group, jump in enumerate(jumps):
        copies = [
            pltpu.make_async_remote_copy(
                src_ref=out_send.at[target],
                dst_ref=out_recv.at[group, c],
                send_sem=b_send.at[group, i],
                recv_sem=b_recv.at[group, c],
                device_id={"ctx": target, "ch": plane(jump)},
                device_id_type=MESH,
            )
            for i, target in enumerate(targets + ([c] if jump else []))
        ]
        b_copies.append(copies)
    for copies in b_copies:
        for copy in copies:
            copy.start()
        sent += copies
    out_recv[4, c] = out_send[c]

    near = y // 2

    def hop(height, half, send_sem, recv_sem, index, target, side=0):
        first = 0 if half is None else pl.multiple_of((near + half) % 2 * 16, 16)
        rows = pl.ds(first, 32 if half is None else 16)
        return pltpu.make_async_remote_copy(
            src_ref=gath.at[0, height, rows],
            dst_ref=gath.at[side, height, rows],
            send_sem=send_sem.at[index],
            recv_sem=recv_sem.at[index],
            device_id={"ch": target},
            device_id_type=MESH,
        )

    def begin(copy):
        copy.start()
        sent.append(copy)

    def share(index, height, half=None):
        begin(hop(height, half, pair_send, pair_recv, index, partner, 1))

    def landed(group, source):
        pltpu.make_async_remote_copy(
            src_ref=out_send.at[0],
            dst_ref=out_recv.at[group, source],
            send_sem=b_send.at[group, 0],
            recv_sem=b_recv.at[group, source],
            device_id={"ctx": targets[0], "ch": h},
            device_id_type=MESH,
        ).wait_recv()

    for half in range(2):
        part = (near + half) % 2
        for group, jump in ((0, 2), (1, -2)):
            for member in range(8):
                landed(group, part * 8 + member)
            height = (z + ROUND - jump) % ROUND
            piece = out_recv[group, pl.ds(part * 8, 8)].astype(jnp.float32)
            rows = wide.at[pl.ds(group * SIDE, SIDE)]
            rows[...] = piece.reshape(SIDE, SIDE)
            first = pl.multiple_of(part * 16, 16)
            for row in range(8):
                gath[0, height, pl.ds(first, 16), row * SIDE : (row + 1) * SIDE] = rows[
                    pl.ds(row, 16, stride=8), :
                ].astype(jnp.bfloat16)
            for side in range(1 + half):
                across = side * (partner - h)
                if half == group:
                    index = 4 + half + 2 * side
                    begin(hop(height, half, z_send, z_recv, index, plane(jump) + across, side))
                index = 2 * half + group if side == 0 else 8 + group
                begin(hop(height, half, z_send, z_recv, index, plane(jump // 2) + across, side))
    for group in (2, 3, 4):
        jump = jumps[group]
        for source in sources if jump == 0 else sources + [c]:
            landed(group, source)
        height = (z + ROUND - jump) % ROUND
        wide[...] = out_recv[group].astype(jnp.float32).reshape(2 * SIDE, SIDE)
        for row in range(8):
            gath[0, height, :, row * SIDE : (row + 1) * SIDE] = wide[
                pl.ds(row, 32, stride=8), :
            ].astype(jnp.bfloat16)
    for group, jump in enumerate(jumps):
        share(group, (z + ROUND - jump) % ROUND)
    arrivals = ((0, -3, 0), (1, 3, 0), (4, 4, 0), (2, -3, 1), (3, 3, 1), (5, 4, 1))
    for order, (index, jump, half) in enumerate(arrivals):
        height = (z + ROUND + jump) % ROUND
        hop(height, half, z_send, z_recv, index, plane(1)).wait_recv()
        if half == 0:
            share(5 + order, height, half)
    columns = [slice(i * CHUNK, (i + 1) * CHUNK) for i in range(1024 // CHUNK)]
    for lanes in columns:
        total[:, lanes] = mm(picked[:, :256], gath[0, :, :, lanes].reshape(256, CHUNK))
    for index in range(8):
        half = None if index < 5 else 0
        hop(z, half, pair_send, pair_recv, index, partner, 1).wait_recv()
    for index in (8, 9, 7):
        hop(z, 1, z_send, z_recv, index, partner, 1).wait_recv()
    for lanes in columns:
        rest = mm(picked[:, 256:], gath[1, :, :, lanes].reshape(256, CHUNK))
        out[:, lanes] = (total[:, lanes] + rest).astype(jnp.bfloat16)
    for copy in sent:
        copy.wait_send()


def solution(mesh):
    consts = tables()
    dma = pltpu.SemaphoreType.DMA
    peers = NODES - 1

    def local(qkv, short_taps, long_filter, skip_gain, out_weight):
        operands = [qkv, jnp.swapaxes(short_taps, 1, 2), long_filter, skip_gain, out_weight]
        operands += [jnp.asarray(t) for t in consts]
        return pl.pallas_call(
            kernel,
            out_shape=jax.ShapeDtypeStruct((512, 1024), jnp.bfloat16),
            in_specs=[pl.BlockSpec(memory_space=pltpu.HBM)] * 10,
            out_specs=pl.BlockSpec(memory_space=pltpu.VMEM),
            scratch_shapes=[
                pltpu.VMEM((3, 32, 1024), jnp.bfloat16),
                pltpu.VMEM((3, TAPS, 32), jnp.float32),
                pltpu.VMEM((32, 1024), jnp.float32),
                pltpu.SMEM((32,), jnp.float32),
                pltpu.VMEM((256, 256), jnp.bfloat16),
                pltpu.VMEM((2, SIDE, SIDE), jnp.float32),
                pltpu.VMEM((2, 256, 256), jnp.bfloat16),
                pltpu.VMEM((2, 256, 256), jnp.bfloat16),
                pltpu.VMEM((2, SIDE, 256), jnp.bfloat16),
                pltpu.VMEM((512, 512), jnp.bfloat16),
                pltpu.VMEM((512, 512), jnp.bfloat16),
                pltpu.VMEM((2, ROUND, 32, 1024), jnp.bfloat16),
                pltpu.VMEM((512, 1024), jnp.float32),
                pltpu.VMEM((256, SIDE), jnp.float32),
                pltpu.VMEM((NODES, 4, 16, SIDE), jnp.bfloat16),
                pltpu.VMEM((NODES, 4, 16, SIDE), jnp.bfloat16),
                pltpu.VMEM((NODES, 16, SIDE), jnp.bfloat16),
                pltpu.VMEM((5, NODES, 16, SIDE), jnp.bfloat16),
                dma((2,)),
                dma((8,)),
                dma((peers,)),
                dma((peers,)),
                dma((peers,)),
                dma((peers,)),
                dma((5, NODES)),
                dma((5, NODES)),
                dma((10,)),
                dma((10,)),
                dma((8,)),
                dma((8,)),
                pltpu.SemaphoreType.REGULAR,
            ],
            compiler_params=pltpu.CompilerParams(
                collective_id=0, has_side_effects=True, vmem_limit_bytes=GRANT
            ),
        )(*[pltpu.with_memory_space_constraint(v, pltpu.HBM) for v in operands])

    placed = (P(None, "ch", "ctx"), P(None, "ch", None), P("ch", "ctx"), P("ch"), P("ch", None))
    return jax.shard_map(
        local, mesh=mesh, in_specs=placed, out_specs=P("ch", "ctx"), check_vma=False
    )
```
